768 devices in a mesh: occ: 16 (over y, core), vir: 48 (over x, z).
Axes of the slice: x: 4, y: 8, z: 12, core: 2. Of those that a mesh axis runs over, the one named last changes fastest.
Arguments:
- amplitudes: bfloat16 [2, 192, 1152, 1152], P(None, 'occ', 'vir'), may hold values from -6 to 6
- integrals: bfloat16 [2, 1152, 1152], P(None, 'vir'), may hold values from -0.1875 to 0.1875
- block_mask: int32 [2, 6, 6], replicated, may hold values 0 or 1
- residual_in: float32 [192, 1152, 1152], P('occ', 'vir'), may hold values from -6 to 6
Outputs:
- residual_out: float32 [192, 1152, 1152], P('occ', 'vir')
The draws below stay inside these ranges and needn't reach their ends.
All inputs are finite; a program needn't handle non-finite values.
Results may differ from the reference program's by a relative error of at most 0.0028.
Values may be sent and summed in bfloat16 or wider, within the bound.
No kernel may reach another device: no remote copies, remote signals or barrier semaphores. Data moves between devices by JAX's collectives and lax.ppermute only.
A program may use at most 128 MiB of HBM per device.

```python
import jax
import jax.numpy as jnp

V = 1152
TILE = 192
KS = 2
NOCC = 192
NT = 6


def plant(values, stream_key, low, high):
    longest = values.shape.index(max(values.shape))
    spots = []
    for shift in (0, 1):
        where = [jax.random.randint(jax.random.fold_in(stream_key, axis), (), 0, length) for axis, length in enumerate(values.shape)]
        where[longest] = (where[longest] + shift) % values.shape[longest]
        spots.append(tuple(where))
    return values.at[spots[0]].set(low).at[spots[1]].set(high)


def levels(rng, shape, split, least, top_value):
    level, own = 1.0, jax.random.fold_in(rng, 6)
    for axis_at, shards_of in split:
        steps = jnp.exp(jax.random.uniform(jax.random.fold_in(own, axis_at), (shards_of,), jnp.float32, least / len(split), top_value / len(split)))
        level = level * jnp.repeat(steps, shape[axis_at] // shards_of).reshape([-1 if axis == axis_at else 1 for axis in range(len(shape))])
    return level


def noise(rng, dims, spread, most, split=(), held_as=jnp.bfloat16):
    entries = spread * jax.random.normal(rng, dims, jnp.float32)
    if split:
        entries = entries * levels(rng, dims, split, -0.22, 0.18)
    return jnp.clip(entries, -most, most).astype(held_as)


def setup_inputs(seed: int = 0) -> dict:
    keys = jax.random.split(jax.random.key(seed), 5)
    amplitudes = noise(keys[0], (KS, NOCC, V, V), 1.0, 6.0, ((1, 16), (2, 48)))
    integrals = noise(keys[1], (KS, V, V), V ** -0.5, 0.1875, ((1, 48),))
    block_mask = plant((jax.random.randint(keys[2], (KS, NT, NT), 0, 2) < 1).astype(jnp.int32), jax.random.fold_in(keys[2], 1), 0, 1)
    residual_in = noise(keys[3], (NOCC, V, V), 1.0, 6.0, ((0, 16), (1, 48)), jnp.float32)
    return {"amplitudes": amplitudes, "integrals": integrals, "block_mask": block_mask, "residual_in": residual_in}


def reference(amplitudes, integrals, block_mask, residual_in):
    expanded = jnp.repeat(jnp.repeat(block_mask.astype(jnp.float32), TILE, axis=1), TILE, axis=2)
    masked = (integrals.astype(jnp.float32) * expanded).astype(jnp.bfloat16)
    result = residual_in
    for cycle_index in range(KS):
        slab_amps = amplitudes[cycle_index]
        combined = (2.0 * slab_amps.astype(jnp.float32) - jnp.swapaxes(slab_amps, 1, 2).astype(jnp.float32)).astype(jnp.bfloat16)
        flat_rows = combined.reshape(NOCC * V, V)
        product = jnp.dot(flat_rows, masked[cycle_index], preferred_element_type=jnp.float32)
        result = result + product.reshape(NOCC, V, V)
    return result
```

```python
import jax
import jax.numpy as jnp
from jax import lax
from jax.experimental import pallas as pl
from jax.experimental.pallas import tpu as pltpu
from jax.sharding import PartitionSpec as P

TILE = 192
LANES = 128
NX, NZ = 4, 12


def pack_body(source, packed, wide):
    pairs, rows, width = source.shape
    peers, tiles = packed.shape[0], packed.shape[1]
    step = width // peers
    wide[...] = source[...].astype(jnp.float32)
    lane = lax.broadcasted_iota(jnp.int32, (rows, LANES), 1)
    for q in range(peers):
        tile, at = divmod(step * q, LANES)
        made = [None] * (tiles + 1)
        for g in range(pairs):
            piece = wide[g, :, tile * LANES : (tile + 1) * LANES]
            if at + step > LANES:
                piece = jnp.where(lane >= at, piece, wide[g, :, (tile + 1) * LANES : (tile + 2) * LANES])
            put, to = divmod(step * g, LANES)
            if to != at:
                piece = pltpu.roll(piece, (to - at) % LANES, 1)
            made[put] = piece if made[put] is None else jnp.where(lane >= to, piece, made[put])
            if to + step > LANES:
                made[put + 1] = piece
        for d in range(tiles):
            packed[q, d] = made[d].astype(jnp.bfloat16)


def pack(amplitudes, peers):
    pairs, rows, width = amplitudes.shape
    step = width // peers
    tiles = -(-pairs * step // LANES)
    blocks = width // 384
    return pl.pallas_call(
        pack_body,
        grid=(blocks,),
        in_specs=[pl.BlockSpec((pairs, rows, 384), lambda p: (0, 0, p))],
        out_specs=pl.BlockSpec((peers // blocks, tiles, rows, LANES), lambda p: (p, 0, 0, 0)),
        out_shape=jax.ShapeDtypeStruct((peers, tiles, rows, LANES), jnp.bfloat16),
        scratch_shapes=[pltpu.VMEM((pairs, rows, 384), jnp.float32)],
        compiler_params=pltpu.CompilerParams(vmem_limit_bytes=40 << 20),
        name="pack",
    )(amplitudes)


def final_body(where, mask, amplitudes, swapped, residual, *rest):
    pieces, out, combined, weights, mask_rows = rest[:-4], rest[-4], rest[-3], rest[-2], rest[-1]
    kept, rows = weights.shape[0], weights.shape[1]
    tiles = rows // TILE
    lane = lax.broadcasted_iota(jnp.int32, (16, rows), 1)
    for k in range(kept):
        for t in range(tiles):
            row = jnp.zeros((16, rows), jnp.float32)
            for u in range(tiles):
                inside = (lane >= u * TILE) & (lane < (u + 1) * TILE)
                row = jnp.where(inside, mask[(k * tiles + t) * tiles + u].astype(jnp.float32), row)
            mask_rows[k * tiles + t] = row.astype(jnp.bfloat16)
    core, mine = where[0], where[1]
    half = pieces[0].shape[0]
    own = half // 2
    spots = [(0, 0), (NX - 1, 0), (1, 0), (NX - 2, 0), (NX - 2, own)]
    for side in range(2):
        k = core if side == 0 else 1 - core
        for at, (shift, start) in enumerate(spots):
            piece = pieces[side * len(spots) + at]
            base = lax.rem(mine + shift, NX) * half + start
            for part in range(piece.shape[0] // 48):
                row = base + part * 48
                tile_row = mask_rows[k * tiles + row // TILE]
                for sub in range(3):
                    spot = part * 48 + sub * 16
                    weights[k, pl.ds(pl.multiple_of(base + spot, 16), 16), :] = piece[spot : spot + 16, :] * tile_row
    pairs = amplitudes.shape[0]
    for d in range(swapped.shape[1]):
        count = min(LANES, pairs - d * LANES)
        turned = jnp.transpose(swapped[:, d].reshape(rows, LANES).astype(jnp.float32))
        own_rows = amplitudes[d * LANES : d * LANES + count, :].astype(jnp.float32)
        combined[d * LANES : d * LANES + count, :] = (2.0 * own_rows - turned[:count]).astype(jnp.bfloat16)
    half_rows = pairs // kept
    out[...] = (
        residual[...]
        + jnp.dot(combined[:half_rows, :], weights[0], preferred_element_type=jnp.float32)
        + jnp.dot(combined[half_rows:, :], weights[1], preferred_element_type=jnp.float32)
    )


def per_device(amplitudes, integrals, block_mask, residual_in):
    kept, occ, rows, width = amplitudes.shape
    core = lax.rem(lax.axis_index("occ"), 2)
    column = lax.div(lax.axis_index("vir"), NZ)
    flat = amplitudes.reshape(kept * occ, rows, width)
    packed = pack(flat, width // rows)
    swapped = lax.all_to_all(packed, "vir", 0, 0, tiled=True)

    along = NX * NZ
    slab = jnp.where(core == 0, integrals[0], integrals[1])
    groups = [[x * NZ + z for z in range(NZ)] for x in range(NX)]
    here = lax.all_gather(slab, "vir", axis=0, tiled=True, axis_index_groups=groups)
    up = [(v, (v + NZ) % along) for v in range(along)]
    down = [(v, (v - NZ) % along) for v in range(along)]
    left = lax.ppermute(here, "vir", up)
    right = lax.ppermute(here, "vir", down)
    half = here.shape[0] // 2
    far_low = lax.ppermute(left[:half], "vir", up)
    far_high = lax.ppermute(right[half:], "vir", down)
    pieces = [here, left, right, far_low, far_high]
    swap_cores = [(j, j ^ 1) for j in range(16)]
    pieces += [lax.ppermute(piece, "occ", swap_cores) for piece in pieces]

    where = jnp.stack([core, column]).astype(jnp.int32)
    flat_rows = kept * occ * rows
    smem = pl.BlockSpec(memory_space=pltpu.SMEM)
    vmem = pl.BlockSpec(memory_space=pltpu.VMEM)
    out = pl.pallas_call(
        final_body,
        in_specs=[smem, smem] + [vmem] * (3 + len(pieces)),
        out_specs=vmem,
        out_shape=jax.ShapeDtypeStruct((occ * rows, width), jnp.float32),
        scratch_shapes=[
            pltpu.VMEM((flat_rows, width), jnp.bfloat16),
            pltpu.VMEM((kept, width, width), jnp.bfloat16),
            pltpu.VMEM((kept * (width // TILE), 16, width), jnp.bfloat16),
        ],
        compiler_params=pltpu.CompilerParams(vmem_limit_bytes=56 << 20),
        name="final",
    )(
        where,
        block_mask.reshape(-1),
        amplitudes.reshape(flat_rows, width),
        swapped,
        residual_in.reshape(occ * rows, width),
        *pieces,
    )
    return out.reshape(residual_in.shape)


def solution(mesh):
    return jax.shard_map(
        per_device,
        mesh=mesh,
        in_specs=(P(None, "occ", "vir", None), P(None, "vir", None), P(), P("occ", "vir", None)),
        out_specs=P("occ", "vir", None),
        check_vma=False,
    )
```

```python
import jax
import jax.numpy as jnp
from jax import lax
from jax.experimental import pallas as pl
from jax.experimental.pallas import tpu as pltpu
from jax.sharding import PartitionSpec as P

TILE = 192
LANES = 128
NX, NZ = 4, 12


def pack_body(source, packed, wide):
    pairs, rows, width = source.shape
    peers = packed.shape[0]
    step = width // peers
    full = pairs * step // LANES
    wide[...] = source[...].astype(jnp.float32)
    lane = lax.broadcasted_iota(jnp.int32, (rows, LANES), 1)
    for q in range(peers):
        tile, at = divmod(step * q, LANES)
        made = [None] * (full + 2)
        for g in range(pairs):
            piece = wide[g, :, tile * LANES : (tile + 1) * LANES]
            if at + step > LANES:
                piece = jnp.where(lane >= at, piece, wide[g, :, (tile + 1) * LANES : (tile + 2) * LANES])
            put, to = divmod(step * g, LANES)
            if to != at:
                piece = pltpu.roll(piece, (to - at) % LANES, 1)
            made[put] = piece if made[put] is None else jnp.where(lane >= to, piece, made[put])
            if to + step > LANES:
                made[put + 1] = piece
        for d in range(full):
            packed[q, d * rows : (d + 1) * rows] = made[d].astype(jnp.bfloat16)
        low, middle, high = (made[full][8 * j : 8 * j + 8] for j in range(3))
        low = jnp.where(lane[:8] < LANES // 2, low, pltpu.roll(middle, LANES // 2, 1))
        packed[q, full * rows :] = jnp.concatenate([low, high], axis=0).astype(jnp.bfloat16)


def pack(amplitudes, peers):
    pairs, rows, width = amplitudes.shape
    full = pairs * (width // peers) // LANES
    tall = full * rows + 16
    blocks = width // 384
    return pl.pallas_call(
        pack_body,
        grid=(blocks,),
        in_specs=[pl.BlockSpec((pairs, rows, 384), lambda p: (0, 0, p))],
        out_specs=pl.BlockSpec((peers // blocks, tall, LANES), lambda p: (p, 0, 0)),
        out_shape=jax.ShapeDtypeStruct((peers, tall, LANES), jnp.bfloat16),
        scratch_shapes=[pltpu.VMEM((pairs, rows, 384), jnp.float32)],
        compiler_params=pltpu.CompilerParams(vmem_limit_bytes=12 << 20),
        name="pack",
    )(amplitudes)


def final_body(where, mask, amplitudes, residual, swapped, *rest):
    pieces, (out, own, combined, weights, start, made, mask_rows, sems) = rest[:-8], rest[-8:]
    kept, width = weights.shape[0], weights.shape[1]
    tiles = width // TILE
    core, mine = where[0], where[1]
    half = pieces[0].shape[0]
    copies = [pltpu.make_async_copy(amplitudes, own, sems.at[0])]
    spots = [(0, 0), (NX - 1, 0), (1, 0), (NX - 2, 0), (NX - 2, half // 2)]
    for side in range(2):
        k = core if side == 0 else 1 - core
        for at, (shift, first) in enumerate(spots):
            piece = pieces[side * len(spots) + at]
            base = pl.multiple_of(lax.rem(mine + shift, NX) * half + first, 16)
            target = weights.at[k, pl.ds(base, piece.shape[0]), :]
            copies.append(pltpu.make_async_copy(piece, target, sems.at[len(copies)]))
    copies.append(pltpu.make_async_copy(residual, start, sems.at[len(copies)]))
    for copy in copies:
        copy.start()

    lane = lax.broadcasted_iota(jnp.int32, (16, width), 1)
    for k in range(kept):
        for t in range(tiles):
            row = jnp.zeros((16, width), jnp.float32)
            for u in range(tiles):
                inside = (lane >= u * TILE) & (lane < (u + 1) * TILE)
                row = jnp.where(inside, mask[(k * tiles + t) * tiles + u].astype(jnp.float32), row)
            mask_rows[k * tiles + t] = row.astype(jnp.bfloat16)

    copies[0].wait()
    pairs = own.shape[0]
    peers, tall = swapped.shape[0], swapped.shape[1]
    rows = width // peers
    full = tall // rows
    for d in range(full + 1):
        count = min(LANES, pairs - d * LANES)
        if d < full:
            tile = swapped[:, d * rows : (d + 1) * rows, :].astype(jnp.float32)
        else:
            ends = swapped[:, d * rows :, :].astype(jnp.float32)
            low = ends[:, :8].reshape(peers * 8, LANES)
            middle = pltpu.roll(low, LANES // 2, 1).reshape(peers, 8, LANES)
            tile = jnp.concatenate([ends[:, :8], middle, ends[:, 8:]], axis=1)
        turned = jnp.transpose(tile.reshape(width, LANES))
        own_rows = own[d * LANES : d * LANES + count, :].astype(jnp.float32)
        combined[d * LANES : d * LANES + count, :] = (2.0 * own_rows - turned[:count]).astype(jnp.bfloat16)

    for copy in copies[1:]:
        copy.wait()
    half_rows = pairs // kept
    wide = 384
    stores = []
    for n in range(width // wide):
        cols = slice(n * wide, (n + 1) * wide)
        total = start[:, cols]
        for k in range(kept):
            masked = jnp.concatenate(
                [
                    (weights[k, t * TILE : (t + 1) * TILE, cols].reshape(-1, 16, wide) * mask_rows[k * tiles + t, :, cols][None])
                    for t in range(tiles)
                ]
            ).reshape(width, wide)
            total += jnp.dot(
                combined[k * half_rows : (k + 1) * half_rows, :], masked, preferred_element_type=jnp.float32
            )
        made[:, cols] = total
        stores.append(pltpu.make_async_copy(made.at[:, cols], out.at[:, cols], sems.at[len(copies) + n]))
        stores[-1].start()
    for store in stores:
        store.wait()


def final(where, mask, amplitudes, residual, swapped, pieces, kept):
    width = residual.shape[1]
    smem = pl.BlockSpec(memory_space=pltpu.SMEM)
    vmem = pl.BlockSpec(memory_space=pltpu.VMEM)
    hbm = pl.BlockSpec(memory_space=pltpu.HBM)
    return pl.pallas_call(
        final_body,
        in_specs=[smem, smem, hbm, hbm, vmem] + [hbm] * len(pieces),
        out_specs=hbm,
        out_shape=jax.ShapeDtypeStruct(residual.shape, jnp.float32),
        scratch_shapes=[
            pltpu.VMEM(amplitudes.shape, jnp.bfloat16),
            pltpu.VMEM(amplitudes.shape, jnp.bfloat16),
            pltpu.VMEM((kept, width, width), jnp.bfloat16),
            pltpu.VMEM(residual.shape, jnp.float32),
            pltpu.VMEM(residual.shape, jnp.float32),
            pltpu.VMEM((kept * (width // TILE), 16, width), jnp.bfloat16),
            pltpu.SemaphoreType.DMA((len(pieces) + 2 + width // 384,)),
        ],
        compiler_params=pltpu.CompilerParams(vmem_limit_bytes=24 << 20),
        name="final",
    )(where, mask, amplitudes, residual, swapped, *pieces)


def per_device(amplitudes, integrals, block_mask, residual_in):
    kept, occ, rows, width = amplitudes.shape
    core = lax.rem(lax.axis_index("occ"), 2)
    column = lax.div(lax.axis_index("vir"), NZ)
    where = jnp.stack([core, column]).astype(jnp.int32)

    along = NX * NZ
    slab = jnp.where(core == 0, integrals[0], integrals[1])
    groups = [[x * NZ + z for z in range(NZ)] for x in range(NX)]
    here = lax.all_gather(slab, "vir", axis=0, tiled=True, axis_index_groups=groups)

    flat, here = lax.optimization_barrier((amplitudes.reshape(kept * occ, rows, width), here))
    packed = pack(pltpu.with_memory_space_constraint(flat, pltpu.HBM), width // rows)
    swapped = lax.all_to_all(packed, "vir", 0, 0, tiled=True)

    up = [(v, (v + NZ) % along) for v in range(along)]
    down = [(v, (v - NZ) % along) for v in range(along)]
    left = lax.ppermute(here, "vir", up)
    right = lax.ppermute(here, "vir", down)
    half = here.shape[0] // 2
    far_low = lax.ppermute(left[:half], "vir", up)
    far_high = lax.ppermute(right[half:], "vir", down)
    pieces = [here, left, right, far_low, far_high]
    swap_cores = [(j, j ^ 1) for j in range(16)]
    pieces += [lax.ppermute(piece, "occ", swap_cores) for piece in pieces]

    out = final(
        where,
        block_mask.reshape(-1),
        pltpu.with_memory_space_constraint(amplitudes.reshape(kept * occ * rows, width), pltpu.HBM),
        pltpu.with_memory_space_constraint(residual_in.reshape(occ * rows, width), pltpu.HBM),
        swapped,
        pieces,
        kept,
    )
    return out.reshape(residual_in.shape)


def solution(mesh):
    return jax.shard_map(
        per_device,
        mesh=mesh,
        in_specs=(P(None, "occ", "vir", None), P(None, "vir", None), P(), P("occ", "vir", None)),
        out_specs=P("occ", "vir", None),
        check_vma=False,
    )
```

```python
import jax
import jax.numpy as jnp
from jax import lax
from jax.experimental import pallas as pl
from jax.experimental.pallas import tpu as pltpu
from jax.sharding import PartitionSpec as P

TILE = 192
LANES = 128
NX, NZ = 4, 12


SPLIT = 6


def in_hbm(array):
    return pltpu.with_memory_space_constraint(array, pltpu.HBM)


def pack_body(source, gathered, packed, narrow, wide, made, sems):
    pairs, rows, width = source.shape
    peers = packed.shape[0]
    step = width // peers
    full = pairs * step // LANES
    part = pairs // SPLIT
    loads = [
        pltpu.make_async_copy(source.at[pl.ds(j * part, part)], narrow.at[pl.ds(j * part, part)], sems.at[j])
        for j in range(SPLIT)
    ]
    for load in loads:
        load.start()
    for j in range(SPLIT):
        loads[j].wait()
        wide[j * part : (j + 1) * part] = narrow[j * part : (j + 1) * part].astype(jnp.float32)
    lane = lax.broadcasted_iota(jnp.int32, (rows, LANES), 1)
    block = 3 * LANES
    many = block // step

    def store(p):
        span = pl.ds(p * many, many)
        return pltpu.make_async_copy(made.at[span], packed.at[span], sems.at[SPLIT + p])

    def fill(p, carry):
        for q in range(many):
            tile, at = divmod(step * q, LANES)
            here = pl.ds(pl.multiple_of(p * block + tile * LANES, LANES), LANES)
            next_tile = pl.ds(pl.multiple_of(p * block + (tile + 1) * LANES, LANES), LANES)
            parts = [None] * (full + 2)
            for g in range(pairs):
                piece = wide[g, :, here]
                if at + step > LANES:
                    piece = jnp.where(lane >= at, piece, wide[g, :, next_tile])
                put, to = divmod(step * g, LANES)
                if to != at:
                    piece = pltpu.roll(piece, (to - at) % LANES, 1)
                parts[put] = piece if parts[put] is None else jnp.where(lane >= to, piece, parts[put])
                if to + step > LANES:
                    parts[put + 1] = piece
            for d in range(full):
                made[p * many + q, d * rows : (d + 1) * rows] = parts[d].astype(jnp.bfloat16)
            low, middle, high = (parts[full][8 * j : 8 * j + 8] for j in range(3))
            low = jnp.where(lane[:8] < LANES // 2, low, pltpu.roll(middle, LANES // 2, 1))
            made[p * many + q, full * rows :] = jnp.concatenate([low, high], axis=0).astype(jnp.bfloat16)
        store(p).start()
        return carry

    blocks = width // block
    lax.fori_loop(0, blocks, fill, 0)
    for p in range(blocks):
        store(p).wait()


def pack(amplitudes, gathered, peers):
    pairs, rows, width = amplitudes.shape
    full = pairs * (width // peers) // LANES
    tall = full * rows + 16
    hbm = pl.BlockSpec(memory_space=pltpu.HBM)
    return pl.pallas_call(
        pack_body,
        in_specs=[hbm, hbm],
        out_specs=hbm,
        out_shape=jax.ShapeDtypeStruct((peers, tall, LANES), jnp.bfloat16),
        scratch_shapes=[
            pltpu.VMEM(amplitudes.shape, jnp.bfloat16),
            pltpu.VMEM(amplitudes.shape, jnp.float32),
            pltpu.VMEM((peers, tall, LANES), jnp.bfloat16),
            pltpu.SemaphoreType.DMA((SPLIT + width // 384,)),
        ],
        compiler_params=pltpu.CompilerParams(vmem_limit_bytes=12 << 20),
        name="pack",
    )(in_hbm(amplitudes), in_hbm(gathered))


def spread_body(mask, piece, mask_rows):
    count, _, width = mask_rows.shape
    tiles = width // TILE
    lane = lax.broadcasted_iota(jnp.int32, (16, width), 1)
    for t in range(count):
        row = jnp.zeros((16, width), jnp.float32)
        for u in range(tiles):
            inside = (lane >= u * TILE) & (lane < (u + 1) * TILE)
            row = jnp.where(inside, mask[t * tiles + u].astype(jnp.float32), row)
        mask_rows[t] = row.astype(jnp.bfloat16)


def spread(block_mask, piece, width):
    tiles = width // TILE
    count = block_mask.size // tiles
    return pl.pallas_call(
        spread_body,
        in_specs=[pl.BlockSpec(memory_space=pltpu.SMEM), pl.BlockSpec(memory_space=pltpu.HBM)],
        out_specs=pl.BlockSpec(memory_space=pltpu.VMEM),
        out_shape=jax.ShapeDtypeStruct((count, 16, width), jnp.bfloat16),
        cost_estimate=pl.CostEstimate(flops=25 * 10**9, transcendentals=0, bytes_accessed=count * 32 * width),
        name="spread",
    )(block_mask.reshape(-1), in_hbm(piece))


def final_body(where, amplitudes, residual, masks, swapped, *rest):
    pieces, (out, own, combined, weights, start, made, mask_rows, sems) = rest[:-8], rest[-8:]
    kept, width = weights.shape[0], weights.shape[1]
    tiles = width // TILE
    core, mine = where[0], where[1]
    half = pieces[0].shape[0]
    copies = [pltpu.make_async_copy(amplitudes, own, sems.at[0])]
    steps = len(pieces) // kept
    for side in range(kept):
        k = core if side == 0 else 1 - core
        for j in range(steps):
            piece = pieces[side * steps + j]
            base = pl.multiple_of(lax.rem(mine + jnp.where(k == 0, NX - j, j), NX) * half, 16)
            target = weights.at[k, pl.ds(base, half), :]
            copies.append(pltpu.make_async_copy(piece, target, sems.at[len(copies)]))
    copies.append(pltpu.make_async_copy(masks, mask_rows, sems.at[len(copies)]))
    copies.append(pltpu.make_async_copy(residual, start, sems.at[len(copies)]))
    for copy in copies:
        copy.start()

    copies[0].wait()
    pairs = own.shape[0]
    peers, tall = swapped.shape[0], swapped.shape[1]
    rows = width // peers
    full = tall // rows
    for d in range(full + 1):
        count = min(LANES, pairs - d * LANES)
        if d < full:
            tile = swapped[:, d * rows : (d + 1) * rows, :].astype(jnp.float32)
        else:
            ends = swapped[:, d * rows :, :].astype(jnp.float32)
            low = ends[:, :8].reshape(peers * 8, LANES)
            middle = pltpu.roll(low, LANES // 2, 1).reshape(peers, 8, LANES)
            tile = jnp.concatenate([ends[:, :8], middle, ends[:, 8:]], axis=1)
        turned = jnp.transpose(tile.reshape(width, LANES))
        own_rows = own[d * LANES : d * LANES + count, :].astype(jnp.float32)
        combined[d * LANES : d * LANES + count, :] = (2.0 * own_rows - turned[:count]).astype(jnp.bfloat16)

    for copy in copies[1:]:
        copy.wait()
    half_rows = pairs // kept
    wide = 384
    stores = []
    for n in range(width // wide):
        cols = slice(n * wide, (n + 1) * wide)
        total = start[:, cols]
        for k in range(kept):
            masked = jnp.concatenate(
                [
                    (weights[k, t * TILE : (t + 1) * TILE, cols].reshape(-1, 16, wide) * mask_rows[k * tiles + t, :, cols][None])
                    for t in range(tiles)
                ]
            ).reshape(width, wide)
            total += jnp.dot(
                combined[k * half_rows : (k + 1) * half_rows, :], masked, preferred_element_type=jnp.float32
            )
        made[:, cols] = total
        stores.append(pltpu.make_async_copy(made.at[:, cols], out.at[:, cols], sems.at[len(copies) + n]))
        stores[-1].start()
    for store in stores:
        store.wait()


def final(where, amplitudes, residual, mask_rows, swapped, pieces, kept):
    width = residual.shape[1]
    smem = pl.BlockSpec(memory_space=pltpu.SMEM)
    vmem = pl.BlockSpec(memory_space=pltpu.VMEM)
    hbm = pl.BlockSpec(memory_space=pltpu.HBM)
    return pl.pallas_call(
        final_body,
        in_specs=[smem, hbm, hbm, hbm, vmem] + [hbm] * len(pieces),
        out_specs=hbm,
        out_shape=jax.ShapeDtypeStruct(residual.shape, jnp.float32),
        scratch_shapes=[
            pltpu.VMEM(amplitudes.shape, jnp.bfloat16),
            pltpu.VMEM(amplitudes.shape, jnp.bfloat16),
            pltpu.VMEM((kept, width, width), jnp.bfloat16),
            pltpu.VMEM(residual.shape, jnp.float32),
            pltpu.VMEM(residual.shape, jnp.float32),
            pltpu.VMEM(mask_rows.shape, jnp.bfloat16),
            pltpu.SemaphoreType.DMA((len(pieces) + 3 + width // 384,)),
        ],
        compiler_params=pltpu.CompilerParams(vmem_limit_bytes=24 << 20),
        name="final",
    )(where, amplitudes, residual, mask_rows, swapped, *pieces)


def per_device(amplitudes, integrals, block_mask, residual_in):
    kept, occ, rows, width = amplitudes.shape
    core = lax.rem(lax.axis_index("occ"), 2)
    column = lax.div(lax.axis_index("vir"), NZ)
    where = jnp.stack([core, column]).astype(jnp.int32)

    along = NX * NZ
    occ_axis = lax.axis_size("occ")
    slab = jnp.where(core == 0, integrals[0], integrals[1])
    groups = [[x * NZ + z for z in range(NZ)] for x in range(NX)]
    here = lax.all_gather(slab, "vir", axis=0, tiled=True, axis_index_groups=groups)

    packed = pack(amplitudes.reshape(kept * occ, rows, width), here, width // rows)
    swapped = lax.all_to_all(packed, "vir", 0, 0, tiled=True)

    ring = [
        (o * along + v, o * along + (v + (NZ if o % 2 == 0 else -NZ)) % along) for o in range(occ_axis) for v in range(along)
    ]
    pieces = [here]
    for _ in range(NX - 1):
        pieces.append(lax.ppermute(pieces[-1], ("occ", "vir"), ring))
    mask_rows = spread(block_mask, pieces[1][:16, :LANES], width)
    swap_cores = [(j, j ^ 1) for j in range(occ_axis)]
    pieces += [lax.ppermute(piece, "occ", swap_cores) for piece in pieces]

    out = final(
        where,
        in_hbm(amplitudes.reshape(kept * occ * rows, width)),
        in_hbm(residual_in.reshape(occ * rows, width)),
        in_hbm(mask_rows),
        swapped,
        pieces,
        kept,
    )
    return out.reshape(residual_in.shape)


def solution(mesh):
    return jax.shard_map(
        per_device,
        mesh=mesh,
        in_specs=(P(None, "occ", "vir", None), P(None, "vir", None), P(), P("occ", "vir", None)),
        out_specs=P("occ", "vir", None),
        check_vma=False,
    )
```

```python
import jax
import jax.numpy as jnp
from jax import lax
from jax.experimental import pallas as pl
from jax.experimental.pallas import tpu as pltpu
from jax.sharding import PartitionSpec as P

TILE = 192
LANES = 128
NX, NZ = 4, 12


def in_hbm(array):
    return pltpu.with_memory_space_constraint(array, pltpu.HBM)


def pack_body(source, gathered, packed, wide):
    pairs, rows, width = source.shape
    peers = packed.shape[0]
    step = width // peers
    full = pairs * step // LANES
    wide[...] = source[...].astype(jnp.float32)
    lane = lax.broadcasted_iota(jnp.int32, (rows, LANES), 1)
    for q in range(peers):
        tile, at = divmod(step * q, LANES)
        made = [None] * (full + 2)
        beside = None
        for g in range(pairs):
            piece = wide[g, :, tile * LANES : (tile + 1) * LANES]
            if at + step > LANES:
                piece = jnp.where(lane >= at, piece, wide[g, :, (tile + 1) * LANES : (tile + 2) * LANES])
            put, to = divmod(step * g, LANES)
            over = step * (g + 1) - full * LANES
            if over > 0:
                first = LANES // 2 + over - step
                turned = pltpu.roll(piece[8:16], (first - at) % LANES, 1)
                beside = turned if beside is None else jnp.where(lane[:8] >= first, turned, beside)
            if to != at:
                piece = pltpu.roll(piece, (to - at) % LANES, 1)
            made[put] = piece if made[put] is None else jnp.where(lane >= to, piece, made[put])
            if to + step > LANES:
                made[put + 1] = piece
        low = jnp.where(lane[:8] < LANES // 2, made[full][:8], beside)
        packed[q] = jnp.concatenate(made[:full] + [low, made[full][16:]], axis=0).astype(jnp.bfloat16)


def pack(amplitudes, gathered, peers):
    pairs, rows, width = amplitudes.shape
    full = pairs * (width // peers) // LANES
    tall = full * rows + 16
    blocks = width // 384
    return pl.pallas_call(
        pack_body,
        grid=(blocks,),
        in_specs=[pl.BlockSpec((pairs, rows, 384), lambda p: (0, 0, p)), pl.BlockSpec(memory_space=pltpu.HBM)],
        out_specs=pl.BlockSpec((peers // blocks, tall, LANES), lambda p: (p, 0, 0)),
        out_shape=jax.ShapeDtypeStruct((peers, tall, LANES), jnp.bfloat16),
        scratch_shapes=[pltpu.VMEM((pairs, rows, 384), jnp.float32)],
        compiler_params=pltpu.CompilerParams(vmem_limit_bytes=12 << 20),
        name="pack",
    )(in_hbm(amplitudes), in_hbm(gathered))


def spread_body(mask, piece, mask_rows):
    count, _, width = mask_rows.shape
    tiles = width // TILE
    lane = lax.broadcasted_iota(jnp.int32, (16, width), 1)
    for t in range(count):
        row = jnp.zeros((16, width), jnp.float32)
        for u in range(tiles):
            inside = (lane >= u * TILE) & (lane < (u + 1) * TILE)
            row = jnp.where(inside, mask[t * tiles + u].astype(jnp.float32), row)
        mask_rows[t] = row.astype(jnp.bfloat16)


def spread(block_mask, piece, width):
    tiles = width // TILE
    count = block_mask.size // tiles
    return pl.pallas_call(
        spread_body,
        in_specs=[pl.BlockSpec(memory_space=pltpu.SMEM), pl.BlockSpec(memory_space=pltpu.HBM)],
        out_specs=pl.BlockSpec(memory_space=pltpu.VMEM),
        out_shape=pltpu.VMEM((count, 16, width), jnp.bfloat16),
        cost_estimate=pl.CostEstimate(flops=25 * 10**9, transcendentals=0, bytes_accessed=count * 32 * width),
        name="spread",
    )(block_mask.reshape(-1), in_hbm(piece))


def final_body(where, own, mask_rows, swapped, residual, *rest):
    pieces, (out, weights, start, combined, made, sems) = rest[:-6], rest[-6:]
    kept, width = weights.shape[0], weights.shape[1]
    tiles = width // TILE
    core, mine = where[0], where[1]
    half = pieces[0].shape[0]
    steps = len(pieces) // kept
    copies = []
    for side in range(kept):
        k = core if side == 0 else 1 - core
        for j in range(steps):
            base = pl.multiple_of(lax.rem(mine + jnp.where(k == 0, NX - j, j), NX) * half, 16)
            target = weights.at[side, pl.ds(base, half), :]
            copies.append(pltpu.make_async_copy(pieces[len(copies)], target, sems.at[len(copies)]))
    copies.append(pltpu.make_async_copy(residual, start, sems.at[len(copies)]))
    for copy in copies:
        copy.start()

    pairs = own.shape[0]
    peers, tall = swapped.shape[0], swapped.shape[1]
    rows = width // peers
    full = tall // rows
    for d in range(full + 1):
        count = min(LANES, pairs - d * LANES)
        if d < full:
            tile = swapped[:, d * rows : (d + 1) * rows, :].astype(jnp.float32)
        else:
            ends = swapped[:, d * rows :, :].astype(jnp.float32)
            low = ends[:, :8].reshape(peers * 8, LANES)
            middle = pltpu.roll(low, LANES // 2, 1).reshape(peers, 8, LANES)
            tile = jnp.concatenate([ends[:, :8], middle, ends[:, 8:]], axis=1)
        turned = jnp.transpose(tile.reshape(width, LANES))
        own_rows = own[d * LANES : d * LANES + count, :].astype(jnp.float32)
        combined[d * LANES : d * LANES + count, :] = (2.0 * own_rows - turned[:count]).astype(jnp.bfloat16)

    half_rows = pairs // kept
    wide = 384
    stores = []
    for side in range(kept):
        k = core if side == 0 else 1 - core
        for copy in copies[side * steps : (side + 1) * steps]:
            copy.wait()
        if side == kept - 1:
            copies[-1].wait()
        left = combined[pl.ds(pl.multiple_of(k * half_rows, 16), half_rows), :]
        for n in range(width // wide):
            cols = slice(n * wide, (n + 1) * wide)
            masked = jnp.concatenate(
                [
                    weights[side, t * TILE : (t + 1) * TILE, cols].reshape(-1, 16, wide)
                    * mask_rows[k * tiles + t, :, cols][None]
                    for t in range(tiles)
                ]
            ).reshape(width, wide)
            total = jnp.dot(left, masked, preferred_element_type=jnp.float32)
            if side == 0:
                made[:, cols] = total
            else:
                made[:, cols] = made[:, cols] + total + start[:, cols]
                stores.append(pltpu.make_async_copy(made.at[:, cols], out.at[:, cols], sems.at[len(copies) + n]))
                stores[-1].start()
    for store in stores:
        store.wait()


def final(where, own, mask_rows, swapped, residual, pieces, kept):
    width = residual.shape[1]
    vmem = pl.BlockSpec(memory_space=pltpu.VMEM)
    hbm = pl.BlockSpec(memory_space=pltpu.HBM)
    return pl.pallas_call(
        final_body,
        in_specs=[pl.BlockSpec(memory_space=pltpu.SMEM)] + [vmem] * 3 + [hbm] * (1 + len(pieces)),
        out_specs=hbm,
        out_shape=jax.ShapeDtypeStruct(residual.shape, jnp.float32),
        scratch_shapes=[
            pltpu.VMEM((kept, width, width), jnp.bfloat16),
            pltpu.VMEM(residual.shape, jnp.float32),
            pltpu.VMEM(own.shape, jnp.bfloat16),
            pltpu.VMEM(residual.shape, jnp.float32),
            pltpu.SemaphoreType.DMA((len(pieces) + 1 + width // 384,)),
        ],
        compiler_params=pltpu.CompilerParams(vmem_limit_bytes=20 << 20),
        name="final",
    )(where, own, mask_rows, swapped, in_hbm(residual), *[in_hbm(piece) for piece in pieces])


def per_device(amplitudes, integrals, block_mask, residual_in):
    kept, occ, rows, width = amplitudes.shape
    core = lax.rem(lax.axis_index("occ"), 2)
    column = lax.div(lax.axis_index("vir"), NZ)
    where = jnp.stack([core, column]).astype(jnp.int32)

    along = NX * NZ
    occ_axis = lax.axis_size("occ")
    slab = jnp.where(core == 0, integrals[0], integrals[1])
    groups = [[x * NZ + z for z in range(NZ)] for x in range(NX)]
    here = lax.all_gather(slab, "vir", axis=0, tiled=True, axis_index_groups=groups)

    packed = pack(amplitudes.reshape(kept * occ, rows, width), here, width // rows)
    swapped = lax.all_to_all(packed, "vir", 0, 0, tiled=True)

    ring = [
        (o * along + v, o * along + (v + (NZ if o % 2 == 0 else -NZ)) % along) for o in range(occ_axis) for v in range(along)
    ]
    pieces = [here]
    for _ in range(NX - 1):
        pieces.append(lax.ppermute(pieces[-1], ("occ", "vir"), ring))
    mask_rows = spread(block_mask, pieces[1][:16, :LANES], width)
    swap_cores = [(j, j ^ 1) for j in range(occ_axis)]
    pieces += [lax.ppermute(piece, "occ", swap_cores) for piece in pieces]

    out = final(
        where,
        amplitudes.reshape(kept * occ * rows, width),
        mask_rows,
        swapped,
        residual_in.reshape(occ * rows, width),
        pieces,
        kept,
    )
    return out.reshape(residual_in.shape)


def solution(mesh):
    return jax.shard_map(
        per_device,
        mesh=mesh,
        in_specs=(P(None, "occ", "vir", None), P(None, "vir", None), P(), P("occ", "vir", None)),
        out_specs=P("occ", "vir", None),
        check_vma=False,
    )
```

```python
import jax
import jax.numpy as jnp
from jax import lax
from jax.experimental import pallas as pl
from jax.experimental.pallas import tpu as pltpu
from jax.sharding import PartitionSpec as P

TILE = 192
LANES = 128
NX, NZ = 4, 12


def in_hbm(array):
    return pltpu.with_memory_space_constraint(array, pltpu.HBM)


def pack_body(source, gathered, packed, wide):
    pairs, rows, width = source.shape
    peers = packed.shape[0]
    step = width // peers
    full = pairs * step // LANES
    wide[...] = source[...].astype(jnp.float32)
    lane = lax.broadcasted_iota(jnp.int32, (rows, LANES), 1)
    for q in range(peers):
        tile, at = divmod(step * q, LANES)
        made = [None] * (full + 2)
        beside = None
        for g in range(pairs):
            piece = wide[g, :, tile * LANES : (tile + 1) * LANES]
            if at + step > LANES:
                piece = jnp.where(lane >= at, piece, wide[g, :, (tile + 1) * LANES : (tile + 2) * LANES])
            put, to = divmod(step * g, LANES)
            over = step * (g + 1) - full * LANES
            if over > 0:
                first = LANES // 2 + over - step
                turned = pltpu.roll(piece[8:16], (first - at) % LANES, 1)
                beside = turned if beside is None else jnp.where(lane[:8] >= first, turned, beside)
            if to != at:
                piece = pltpu.roll(piece, (to - at) % LANES, 1)
            made[put] = piece if made[put] is None else jnp.where(lane >= to, piece, made[put])
            if to + step > LANES:
                made[put + 1] = piece
        low = jnp.where(lane[:8] < LANES // 2, made[full][:8], beside)
        packed[q] = jnp.concatenate(made[:full] + [low, made[full][16:]], axis=0).astype(jnp.bfloat16)


def pack(amplitudes, gathered, peers):
    pairs, rows, width = amplitudes.shape
    full = pairs * (width // peers) // LANES
    tall = full * rows + 16
    blocks = width // 384
    return pl.pallas_call(
        pack_body,
        grid=(blocks,),
        in_specs=[pl.BlockSpec((pairs, rows, 384), lambda p: (0, 0, p)), pl.BlockSpec(memory_space=pltpu.HBM)],
        out_specs=pl.BlockSpec((peers // blocks, tall, LANES), lambda p: (p, 0, 0)),
        out_shape=jax.ShapeDtypeStruct((peers, tall, LANES), jnp.bfloat16),
        scratch_shapes=[pltpu.VMEM((pairs, rows, 384), jnp.float32)],
        compiler_params=pltpu.CompilerParams(vmem_limit_bytes=12 << 20),
        name="pack",
    )(in_hbm(amplitudes), in_hbm(gathered))


def spread_body(mask, piece, mask_rows):
    count, _, width = mask_rows.shape
    tiles = width // TILE
    lane = lax.broadcasted_iota(jnp.int32, (16, width), 1)
    for t in range(count):
        row = jnp.zeros((16, width), jnp.float32)
        for u in range(tiles):
            inside = (lane >= u * TILE) & (lane < (u + 1) * TILE)
            row = jnp.where(inside, mask[t * tiles + u].astype(jnp.float32), row)
        mask_rows[t] = row.astype(jnp.bfloat16)


def spread(block_mask, piece, width):
    tiles = width // TILE
    count = block_mask.size // tiles
    return pl.pallas_call(
        spread_body,
        in_specs=[pl.BlockSpec(memory_space=pltpu.SMEM), pl.BlockSpec(memory_space=pltpu.HBM)],
        out_specs=pl.BlockSpec(memory_space=pltpu.VMEM),
        out_shape=pltpu.VMEM((count, 16, width), jnp.bfloat16),
        cost_estimate=pl.CostEstimate(flops=0, transcendentals=0, bytes_accessed=count * 32 * width),
        name="spread",
    )(block_mask.reshape(-1), in_hbm(piece))


def final_body(where, own, mask_rows, swapped, residual, *rest):
    pieces, (out, weights, start, combined, made, sems) = rest[:-6], rest[-6:]
    kept, width = weights.shape[0], weights.shape[1]
    tiles = width // TILE
    core, mine = where[0], where[1]
    half = pieces[0].shape[0]
    steps = len(pieces) // kept
    def load(side, j):
        k = core if side == 0 else 1 - core
        base = pl.multiple_of(lax.rem(mine + jnp.where(k == 0, NX - j, j), NX) * half, 16)
        target = weights.at[k, pl.ds(base, half), :]
        return pltpu.make_async_copy(pieces[side * steps + j], target, sems.at[k * steps + j])

    @pl.when(core == 0)
    def _():
        for side in range(kept):
            for j in range(steps):
                load(side, j).start()

    @pl.when(core != 0)
    def _():
        for side in reversed(range(kept)):
            for j in range(steps):
                load(side, j).start()

    rest_load = pltpu.make_async_copy(residual, start, sems.at[kept * steps])
    rest_load.start()

    pairs = own.shape[0]
    peers, tall = swapped.shape[0], swapped.shape[1]
    rows = width // peers
    full = tall // rows
    half_rows = pairs // kept
    wide = 384
    stores = []

    def combine(d):
        count = min(LANES, pairs - d * LANES)
        if d < full:
            tile = swapped[:, d * rows : (d + 1) * rows, :].astype(jnp.float32)
        else:
            ends = swapped[:, d * rows :, :].astype(jnp.float32)
            low = ends[:, :8].reshape(peers * 8, LANES)
            middle = pltpu.roll(low, LANES // 2, 1).reshape(peers, 8, LANES)
            tile = jnp.concatenate([ends[:, :8], middle, ends[:, 8:]], axis=1)
        turned = jnp.transpose(tile.reshape(width, LANES))
        own_rows = own[d * LANES : d * LANES + count, :].astype(jnp.float32)
        combined[d * LANES : d * LANES + count, :] = (2.0 * own_rows - turned[:count]).astype(jnp.bfloat16)

    ready = 0
    for k in range(kept):
        while ready * LANES < (k + 1) * half_rows:
            combine(ready)
            ready += 1
        for j in range(steps):
            pltpu.make_async_copy(
                pieces[0], weights.at[k, pl.ds(j * half, half), :], sems.at[k * steps + j]
            ).wait()
        if k == kept - 1:
            rest_load.wait()
        for n in range(width // wide):
            cols = slice(n * wide, (n + 1) * wide)
            masked = jnp.concatenate(
                [
                    weights[k, t * TILE : (t + 1) * TILE, cols].reshape(-1, 16, wide)
                    * mask_rows[k * tiles + t, :, cols][None]
                    for t in range(tiles)
                ]
            ).reshape(width, wide)
            total = jnp.dot(
                combined[k * half_rows : (k + 1) * half_rows, :], masked, preferred_element_type=jnp.float32
            )
            if k == 0:
                made[:, cols] = total
            else:
                made[:, cols] = made[:, cols] + total + start[:, cols]
                stores.append(pltpu.make_async_copy(made.at[:, cols], out.at[:, cols], sems.at[kept * steps + 1 + n]))
                stores[-1].start()
    for store in stores:
        store.wait()


def final(where, own, mask_rows, swapped, residual, pieces, kept):
    width = residual.shape[1]
    vmem = pl.BlockSpec(memory_space=pltpu.VMEM)
    hbm = pl.BlockSpec(memory_space=pltpu.HBM)
    return pl.pallas_call(
        final_body,
        in_specs=[pl.BlockSpec(memory_space=pltpu.SMEM)] + [vmem] * 3 + [hbm] * (1 + len(pieces)),
        out_specs=hbm,
        out_shape=jax.ShapeDtypeStruct(residual.shape, jnp.float32),
        scratch_shapes=[
            pltpu.VMEM((kept, width, width), jnp.bfloat16),
            pltpu.VMEM(residual.shape, jnp.float32),
            pltpu.VMEM(own.shape, jnp.bfloat16),
            pltpu.VMEM(residual.shape, jnp.float32),
            pltpu.SemaphoreType.DMA((len(pieces) + 1 + width // 384,)),
        ],
        compiler_params=pltpu.CompilerParams(vmem_limit_bytes=20 << 20),
        name="final",
    )(where, own, mask_rows, swapped, in_hbm(residual), *[in_hbm(piece) for piece in pieces])


def per_device(amplitudes, integrals, block_mask, residual_in):
    kept, occ, rows, width = amplitudes.shape
    core = lax.rem(lax.axis_index("occ"), 2)
    column = lax.div(lax.axis_index("vir"), NZ)
    where = jnp.stack([core, column]).astype(jnp.int32)

    along = NX * NZ
    occ_axis = lax.axis_size("occ")
    slab = jnp.where(core == 0, integrals[0], integrals[1])
    groups = [[x * NZ + z for z in range(NZ)] for x in range(NX)]
    here = lax.all_gather(slab, "vir", axis=0, tiled=True, axis_index_groups=groups)

    packed = pack(amplitudes.reshape(kept * occ, rows, width), here, width // rows)
    swapped = lax.all_to_all(packed, "vir", 0, 0, tiled=True)

    def neighbour(array, sign):
        pairs = [
            (o * along + v, o * along + (v + (NZ if o % 2 == 0 else -NZ) * sign) % along)
            for o in range(occ_axis)
            for v in range(along)
        ]
        return lax.ppermute(array, ("occ", "vir"), pairs)

    first = neighbour(here, 1)
    pieces = [here, first, neighbour(first, 1), neighbour(here, -1)]
    mask_rows = spread(block_mask, pieces[1][:16, :LANES], width)
    swap_cores = [(j, j ^ 1) for j in range(occ_axis)]
    pieces += [lax.ppermute(piece, "occ", swap_cores) for piece in pieces]

    out = final(
        where,
        amplitudes.reshape(kept * occ * rows, width),
        mask_rows,
        swapped,
        residual_in.reshape(occ * rows, width),
        pieces,
        kept,
    )
    return out.reshape(residual_in.shape)


def solution(mesh):
    return jax.shard_map(
        per_device,
        mesh=mesh,
        in_specs=(P(None, "occ", "vir", None), P(None, "vir", None), P(), P("occ", "vir", None)),
        out_specs=P("occ", "vir", None),
        check_vma=False,
    )
```

```python
import jax
import jax.numpy as jnp
from jax import lax
from jax.experimental import pallas as pl
from jax.experimental.pallas import tpu as pltpu
from jax.sharding import PartitionSpec as P

TILE = 192
LANES = 128
NX, NZ = 4, 12


def in_hbm(array):
    return pltpu.with_memory_space_constraint(array, pltpu.HBM)


def pack_body(source, gathered, packed, wide):
    pairs, rows, width = source.shape
    peers = packed.shape[0]
    step = width // peers
    full = pairs * step // LANES
    wide[...] = source[...].astype(jnp.float32)
    lane = lax.broadcasted_iota(jnp.int32, (rows, LANES), 1)
    for q in range(peers):
        tile, at = divmod(step * q, LANES)
        made = [None] * (full + 2)
        beside = None
        for g in range(pairs):
            piece = wide[g, :, tile * LANES : (tile + 1) * LANES]
            if at + step > LANES:
                piece = jnp.where(lane >= at, piece, wide[g, :, (tile + 1) * LANES : (tile + 2) * LANES])
            put, to = divmod(step * g, LANES)
            over = step * (g + 1) - full * LANES
            if over > 0:
                first = LANES // 2 + over - step
                turned = pltpu.roll(piece[8:16], (first - at) % LANES, 1)
                beside = turned if beside is None else jnp.where(lane[:8] >= first, turned, beside)
            if to != at:
                piece = pltpu.roll(piece, (to - at) % LANES, 1)
            made[put] = piece if made[put] is None else jnp.where(lane >= to, piece, made[put])
            if to + step > LANES:
                made[put + 1] = piece
        low = jnp.where(lane[:8] < LANES // 2, made[full][:8], beside)
        packed[q] = jnp.concatenate(made[:full] + [low, made[full][16:]], axis=0).astype(jnp.bfloat16)


def pack(amplitudes, gathered, peers):
    pairs, rows, width = amplitudes.shape
    full = pairs * (width // peers) // LANES
    tall = full * rows + 16
    blocks = width // 384
    return pl.pallas_call(
        pack_body,
        grid=(blocks,),
        in_specs=[pl.BlockSpec((pairs, rows, 384), lambda p: (0, 0, p)), pl.BlockSpec(memory_space=pltpu.HBM)],
        out_specs=pl.BlockSpec((peers // blocks, tall, LANES), lambda p: (p, 0, 0)),
        out_shape=jax.ShapeDtypeStruct((peers, tall, LANES), jnp.bfloat16),
        scratch_shapes=[pltpu.VMEM((pairs, rows, 384), jnp.float32)],
        compiler_params=pltpu.CompilerParams(vmem_limit_bytes=12 << 20),
        name="pack",
    )(in_hbm(amplitudes), in_hbm(gathered))


def final_body(where, mask, own, swapped, residual, *rest):
    pieces, (out, weights, start, combined, made, mask_rows, sems) = rest[:-7], rest[-7:]
    kept, width = weights.shape[0], weights.shape[1]
    tiles = width // TILE
    core, mine = where[0], where[1]
    half = pieces[0].shape[0]
    steps = len(pieces) // kept
    def load(side, j):
        k = core if side == 0 else 1 - core
        base = pl.multiple_of(lax.rem(mine + jnp.where(k == 0, NX - j, j), NX) * half, 16)
        target = weights.at[k, pl.ds(base, half), :]
        return pltpu.make_async_copy(pieces[side * steps + j], target, sems.at[k * steps + j])

    @pl.when(core == 0)
    def _():
        for side in range(kept):
            for j in range(steps):
                load(side, j).start()

    @pl.when(core != 0)
    def _():
        for side in reversed(range(kept)):
            for j in range(steps):
                load(side, j).start()

    rest_load = pltpu.make_async_copy(residual, start, sems.at[kept * steps])
    rest_load.start()

    lane = lax.broadcasted_iota(jnp.int32, (16, width), 1)
    for t in range(kept * tiles):
        row = jnp.zeros((16, width), jnp.float32)
        for u in range(tiles):
            inside = (lane >= u * TILE) & (lane < (u + 1) * TILE)
            row = jnp.where(inside, mask[t * tiles + u].astype(jnp.float32), row)
        mask_rows[t] = row.astype(jnp.bfloat16)

    pairs = own.shape[0]
    peers, tall = swapped.shape[0], swapped.shape[1]
    rows = width // peers
    full = tall // rows
    half_rows = pairs // kept
    wide = 384
    stores = []

    def combine(d):
        count = min(LANES, pairs - d * LANES)
        if d < full:
            tile = swapped[:, d * rows : (d + 1) * rows, :].astype(jnp.float32)
        else:
            ends = swapped[:, d * rows :, :].astype(jnp.float32)
            low = ends[:, :8].reshape(peers * 8, LANES)
            middle = pltpu.roll(low, LANES // 2, 1).reshape(peers, 8, LANES)
            tile = jnp.concatenate([ends[:, :8], middle, ends[:, 8:]], axis=1)
        turned = jnp.transpose(tile.reshape(width, LANES))
        own_rows = own[d * LANES : d * LANES + count, :].astype(jnp.float32)
        combined[d * LANES : d * LANES + count, :] = (2.0 * own_rows - turned[:count]).astype(jnp.bfloat16)

    ready = 0
    for k in range(kept):
        while ready * LANES < (k + 1) * half_rows:
            combine(ready)
            ready += 1
        for j in range(steps):
            pltpu.make_async_copy(
                pieces[0], weights.at[k, pl.ds(j * half, half), :], sems.at[k * steps + j]
            ).wait()
        if k == kept - 1:
            rest_load.wait()
        for n in range(width // wide):
            cols = slice(n * wide, (n + 1) * wide)
            masked = jnp.concatenate(
                [
                    weights[k, t * TILE : (t + 1) * TILE, cols].reshape(-1, 16, wide)
                    * mask_rows[k * tiles + t, :, cols][None]
                    for t in range(tiles)
                ]
            ).reshape(width, wide)
            total = jnp.dot(
                combined[k * half_rows : (k + 1) * half_rows, :], masked, preferred_element_type=jnp.float32
            )
            if k == 0:
                made[:, cols] = total
            else:
                made[:, cols] = made[:, cols] + total + start[:, cols]
                stores.append(pltpu.make_async_copy(made.at[:, cols], out.at[:, cols], sems.at[kept * steps + 1 + n]))
                stores[-1].start()
    for store in stores:
        store.wait()


def final(where, mask, own, swapped, residual, pieces, kept):
    width = residual.shape[1]
    smem = pl.BlockSpec(memory_space=pltpu.SMEM)
    vmem = pl.BlockSpec(memory_space=pltpu.VMEM)
    hbm = pl.BlockSpec(memory_space=pltpu.HBM)
    return pl.pallas_call(
        final_body,
        in_specs=[smem] * 2 + [vmem] * 2 + [hbm] * (1 + len(pieces)),
        out_specs=hbm,
        out_shape=jax.ShapeDtypeStruct(residual.shape, jnp.float32),
        scratch_shapes=[
            pltpu.VMEM((kept, width, width), jnp.bfloat16),
            pltpu.VMEM(residual.shape, jnp.float32),
            pltpu.VMEM(own.shape, jnp.bfloat16),
            pltpu.VMEM(residual.shape, jnp.float32),
            pltpu.VMEM((kept * (width // TILE), 16, width), jnp.bfloat16),
            pltpu.SemaphoreType.DMA((len(pieces) + 1 + width // 384,)),
        ],
        compiler_params=pltpu.CompilerParams(vmem_limit_bytes=20 << 20),
        name="final",
    )(where, mask, own, swapped, in_hbm(residual), *[in_hbm(piece) for piece in pieces])


def per_device(amplitudes, integrals, block_mask, residual_in):
    kept, occ, rows, width = amplitudes.shape
    core = lax.rem(lax.axis_index("occ"), 2)
    column = lax.div(lax.axis_index("vir"), NZ)
    where = jnp.stack([core, column]).astype(jnp.int32)

    along = NX * NZ
    occ_axis = lax.axis_size("occ")
    slab = jnp.where(core == 0, integrals[0], integrals[1])
    groups = [[x * NZ + z for z in range(NZ)] for x in range(NX)]
    here = lax.all_gather(slab, "vir", axis=0, tiled=True, axis_index_groups=groups)

    packed = pack(amplitudes.reshape(kept * occ, rows, width), here, width // rows)
    swapped = lax.all_to_all(packed, "vir", 0, 0, tiled=True)

    def neighbour(array, sign):
        pairs = [
            (o * along + v, o * along + (v + (NZ if o % 2 == 0 else -NZ) * sign) % along)
            for o in range(occ_axis)
            for v in range(along)
        ]
        return lax.ppermute(array, ("occ", "vir"), pairs)

    first = neighbour(here, 1)
    first, later = lax.optimization_barrier((first, here))
    pieces = [here, first, neighbour(first, 1), neighbour(later, -1)]
    swap_cores = [(j, j ^ 1) for j in range(occ_axis)]
    pieces += [lax.ppermute(piece, "occ", swap_cores) for piece in pieces]

    out = final(
        where,
        block_mask.reshape(-1),
        amplitudes.reshape(kept * occ * rows, width),
        swapped,
        residual_in.reshape(occ * rows, width),
        pieces,
        kept,
    )
    return out.reshape(residual_in.shape)


def solution(mesh):
    return jax.shard_map(
        per_device,
        mesh=mesh,
        in_specs=(P(None, "occ", "vir", None), P(None, "vir", None), P(), P("occ", "vir", None)),
        out_specs=P("occ", "vir", None),
        check_vma=False,
    )
```

```python
import jax
import jax.numpy as jnp
from jax import lax
from jax.experimental import pallas as pl
from jax.experimental.pallas import tpu as pltpu
from jax.sharding import PartitionSpec as P

TILE = 192
LANES = 128
NX, NZ = 4, 12


def in_hbm(array):
    return pltpu.with_memory_space_constraint(array, pltpu.HBM)


def pack_body(source, gathered, packed, wide):
    pairs, rows, width = source.shape
    peers = packed.shape[0]
    step = width // peers
    full = pairs * step // LANES
    wide[...] = source[...].astype(jnp.float32)
    lane = lax.broadcasted_iota(jnp.int32, (rows, LANES), 1)
    for q in range(peers):
        tile, at = divmod(step * q, LANES)
        made = [None] * (full + 2)
        beside = None
        for g in range(pairs):
            piece = wide[g, :, tile * LANES : (tile + 1) * LANES]
            if at + step > LANES:
                piece = jnp.where(lane >= at, piece, wide[g, :, (tile + 1) * LANES : (tile + 2) * LANES])
            put, to = divmod(step * g, LANES)
            over = step * (g + 1) - full * LANES
            if over > 0:
                first = LANES // 2 + over - step
                turned = pltpu.roll(piece[8:16], (first - at) % LANES, 1)
                beside = turned if beside is None else jnp.where(lane[:8] >= first, turned, beside)
            if to != at:
                piece = pltpu.roll(piece, (to - at) % LANES, 1)
            made[put] = piece if made[put] is None else jnp.where(lane >= to, piece, made[put])
            if to + step > LANES:
                made[put + 1] = piece
        low = jnp.where(lane[:8] < LANES // 2, made[full][:8], beside)
        packed[q] = jnp.concatenate(made[:full] + [low, made[full][16:]], axis=0).astype(jnp.bfloat16)


def pack(amplitudes, gathered, peers):
    pairs, rows, width = amplitudes.shape
    full = pairs * (width // peers) // LANES
    tall = full * rows + 16
    blocks = width // 384
    return pl.pallas_call(
        pack_body,
        grid=(blocks,),
        in_specs=[pl.BlockSpec((pairs, rows, 384), lambda p: (0, 0, p)), pl.BlockSpec(memory_space=pltpu.HBM)],
        out_specs=pl.BlockSpec((peers // blocks, tall, LANES), lambda p: (p, 0, 0)),
        out_shape=jax.ShapeDtypeStruct((peers, tall, LANES), jnp.bfloat16),
        scratch_shapes=[pltpu.VMEM((pairs, rows, 384), jnp.float32)],
        compiler_params=pltpu.CompilerParams(vmem_limit_bytes=12 << 20),
        name="pack",
    )(in_hbm(amplitudes), in_hbm(gathered))


def final_body(where, mask, own, swapped, residual, *rest):
    pieces, (out, weights, start, combined, made, mask_rows, sems) = rest[:-7], rest[-7:]
    kept, width = weights.shape[0], weights.shape[1]
    tiles = width // TILE
    core, mine, half_at = where[0], where[1], where[2]
    half = pieces[0].shape[0]
    steps = len(pieces) // kept
    def load(side, j):
        k = core if side == 0 else 1 - core
        shift = min(j, NX - 1)
        first = 0 if j < NX - 1 else (half_at if j == NX - 1 else 1 - half_at) * (half // 2)
        base = lax.rem(mine + jnp.where(k == 0, NX - shift, shift), NX) * half + first
        piece = pieces[side * steps + j]
        target = weights.at[k, pl.ds(pl.multiple_of(base, 16), piece.shape[0]), :]
        return pltpu.make_async_copy(piece, target, sems.at[k])

    @pl.when(core == 0)
    def _():
        for side in range(kept):
            for j in range(steps):
                load(side, j).start()

    @pl.when(core != 0)
    def _():
        for side in reversed(range(kept)):
            for j in range(steps):
                load(side, j).start()

    rest_load = pltpu.make_async_copy(residual, start, sems.at[kept])
    rest_load.start()

    lane = lax.broadcasted_iota(jnp.int32, (16, width), 1)
    for t in range(kept * tiles):
        row = jnp.zeros((16, width), jnp.float32)
        for u in range(tiles):
            inside = (lane >= u * TILE) & (lane < (u + 1) * TILE)
            row = jnp.where(inside, mask[t * tiles + u].astype(jnp.float32), row)
        mask_rows[t] = row.astype(jnp.bfloat16)

    pairs = own.shape[0]
    peers, tall = swapped.shape[0], swapped.shape[1]
    rows = width // peers
    full = tall // rows
    half_rows = pairs // kept
    wide = 384
    stores = []

    def combine(d):
        count = min(LANES, pairs - d * LANES)
        if d < full:
            tile = swapped[:, d * rows : (d + 1) * rows, :].astype(jnp.float32)
        else:
            ends = swapped[:, d * rows :, :].astype(jnp.float32)
            low = ends[:, :8].reshape(peers * 8, LANES)
            middle = pltpu.roll(low, LANES // 2, 1).reshape(peers, 8, LANES)
            tile = jnp.concatenate([ends[:, :8], middle, ends[:, 8:]], axis=1)
        turned = jnp.transpose(tile.reshape(width, LANES))
        own_rows = own[d * LANES : d * LANES + count, :].astype(jnp.float32)
        combined[d * LANES : d * LANES + count, :] = (2.0 * own_rows - turned[:count]).astype(jnp.bfloat16)

    ready = 0
    for k in range(kept):
        while ready * LANES < (k + 1) * half_rows:
            combine(ready)
            ready += 1
        pltpu.make_async_copy(weights.at[k], weights.at[k], sems.at[k]).wait()
        if k == kept - 1:
            rest_load.wait()
        for n in range(width // wide):
            cols = slice(n * wide, (n + 1) * wide)
            masked = jnp.concatenate(
                [
                    weights[k, t * TILE : (t + 1) * TILE, cols].reshape(-1, 16, wide)
                    * mask_rows[k * tiles + t, :, cols][None]
                    for t in range(tiles)
                ]
            ).reshape(width, wide)
            total = jnp.dot(
                combined[k * half_rows : (k + 1) * half_rows, :], masked, preferred_element_type=jnp.float32
            )
            if k == 0:
                made[:, cols] = total
            else:
                made[:, cols] = made[:, cols] + total + start[:, cols]
                stores.append(pltpu.make_async_copy(made.at[:, cols], out.at[:, cols], sems.at[kept + 1 + n]))
                stores[-1].start()
    for store in stores:
        store.wait()


def final(where, mask, own, swapped, residual, pieces, kept):
    width = residual.shape[1]
    smem = pl.BlockSpec(memory_space=pltpu.SMEM)
    vmem = pl.BlockSpec(memory_space=pltpu.VMEM)
    hbm = pl.BlockSpec(memory_space=pltpu.HBM)
    return pl.pallas_call(
        final_body,
        in_specs=[smem] * 2 + [vmem] * 2 + [hbm] * (1 + len(pieces)),
        out_specs=hbm,
        out_shape=jax.ShapeDtypeStruct(residual.shape, jnp.float32),
        scratch_shapes=[
            pltpu.VMEM((kept, width, width), jnp.bfloat16),
            pltpu.VMEM(residual.shape, jnp.float32),
            pltpu.VMEM(own.shape, jnp.bfloat16),
            pltpu.VMEM(residual.shape, jnp.float32),
            pltpu.VMEM((kept * (width // TILE), 16, width), jnp.bfloat16),
            pltpu.SemaphoreType.DMA((kept + 1 + width // 384,)),
        ],
        compiler_params=pltpu.CompilerParams(vmem_limit_bytes=20 << 20),
        name="final",
    )(where, mask, own, swapped, in_hbm(residual), *[in_hbm(piece) for piece in pieces])


def per_device(amplitudes, integrals, block_mask, residual_in):
    kept, occ, rows, width = amplitudes.shape
    core = lax.rem(lax.axis_index("occ"), 2)
    column = lax.div(lax.axis_index("vir"), NZ)
    plane = lax.rem(lax.div(lax.axis_index("occ"), 2), 2)
    where = jnp.stack([core, column, plane]).astype(jnp.int32)

    along = NX * NZ
    occ_axis = lax.axis_size("occ")
    slab = jnp.where(core == 0, integrals[0], integrals[1])
    groups = [[x * NZ + z for z in range(NZ)] for x in range(NX)]
    here = lax.all_gather(slab, "vir", axis=0, tiled=True, axis_index_groups=groups)

    packed = pack(amplitudes.reshape(kept * occ, rows, width), here, width // rows)
    swapped = lax.all_to_all(packed, "vir", 0, 0, tiled=True)

    def neighbour(array, sign):
        pairs = [
            (o * along + v, o * along + (v + (NZ if o % 2 == 0 else -NZ) * sign) % along)
            for o in range(occ_axis)
            for v in range(along)
        ]
        return lax.ppermute(array, ("occ", "vir"), pairs)

    first = neighbour(here, 1)
    half = here.shape[0] // 2
    near = neighbour(lax.dynamic_slice_in_dim(here, plane * half, half, 0), -1)
    first, near = lax.optimization_barrier((first, near))
    other = lax.ppermute(near, "occ", [(j, j ^ 2) for j in range(occ_axis)])
    pieces = [here, first, neighbour(first, 1), near, other]
    swap_cores = [(j, j ^ 1) for j in range(occ_axis)]
    pieces += [lax.ppermute(piece, "occ", swap_cores) for piece in pieces]

    out = final(
        where,
        block_mask.reshape(-1),
        amplitudes.reshape(kept * occ * rows, width),
        swapped,
        residual_in.reshape(occ * rows, width),
        pieces,
        kept,
    )
    return out.reshape(residual_in.shape)


def solution(mesh):
    return jax.shard_map(
        per_device,
        mesh=mesh,
        in_specs=(P(None, "occ", "vir", None), P(None, "vir", None), P(), P("occ", "vir", None)),
        out_specs=P("occ", "vir", None),
        check_vma=False,
    )
```

```python
import jax
import jax.numpy as jnp
from jax import lax
from jax.experimental import pallas as pl
from jax.experimental.pallas import tpu as pltpu
from jax.sharding import PartitionSpec as P

TILE = 192
LANES = 128
NX, NZ = 4, 12


def in_hbm(array):
    return pltpu.with_memory_space_constraint(array, pltpu.HBM)


def pack_body(source, gathered, packed, wide):
    pairs, rows, width = source.shape
    peers = packed.shape[0]
    step = width // peers
    full = pairs * step // LANES
    wide[...] = source[...].astype(jnp.float32)
    lane = lax.broadcasted_iota(jnp.int32, (rows, LANES), 1)
    for q in range(peers):
        tile, at = divmod(step * q, LANES)
        made = [None] * (full + 2)
        beside = None
        for g in range(pairs):
            piece = wide[g, :, tile * LANES : (tile + 1) * LANES]
            if at + step > LANES:
                piece = jnp.where(lane >= at, piece, wide[g, :, (tile + 1) * LANES : (tile + 2) * LANES])
            put, to = divmod(step * g, LANES)
            over = step * (g + 1) - full * LANES
            if over > 0:
                first = LANES // 2 + over - step
                turned = pltpu.roll(piece[8:16], (first - at) % LANES, 1)
                beside = turned if beside is None else jnp.where(lane[:8] >= first, turned, beside)
            if to != at:
                piece = pltpu.roll(piece, (to - at) % LANES, 1)
            made[put] = piece if made[put] is None else jnp.where(lane >= to, piece, made[put])
            if to + step > LANES:
                made[put + 1] = piece
        low = jnp.where(lane[:8] < LANES // 2, made[full][:8], beside)
        packed[q] = jnp.concatenate(made[:full] + [low, made[full][16:]], axis=0).astype(jnp.bfloat16)


def pack(amplitudes, gathered, peers):
    pairs, rows, width = amplitudes.shape
    full = pairs * (width // peers) // LANES
    tall = full * rows + 16
    blocks = width // 384
    return pl.pallas_call(
        pack_body,
        grid=(blocks,),
        in_specs=[pl.BlockSpec((pairs, rows, 384), lambda p: (0, 0, p)), pl.BlockSpec(memory_space=pltpu.HBM)],
        out_specs=pl.BlockSpec((peers // blocks, tall, LANES), lambda p: (p, 0, 0)),
        out_shape=jax.ShapeDtypeStruct((peers, tall, LANES), jnp.bfloat16),
        scratch_shapes=[pltpu.VMEM((pairs, rows, 384), jnp.float32)],
        compiler_params=pltpu.CompilerParams(vmem_limit_bytes=12 << 20),
        name="pack",
    )(in_hbm(amplitudes), in_hbm(gathered))


def final_body(where, mask, own, swapped, residual, *rest):
    pieces, (out, weights, start, combined, made, mask_rows, sems) = rest[:-7], rest[-7:]
    kept, width = weights.shape[0], weights.shape[1]
    tiles = width // TILE
    core, mine, half_at = where[0], where[1], where[2]
    half = pieces[0].shape[0]
    steps = len(pieces) // kept
    def load(side, j):
        k = core if side == 0 else 1 - core
        shift = min(j, NX - 1)
        first = 0 if j < NX - 1 else (half_at if j == NX - 1 else 1 - half_at) * (half // 2)
        base = lax.rem(mine + jnp.where(k == 0, NX - shift, shift), NX) * half + first
        piece = pieces[side * steps + j]
        target = weights.at[k, pl.ds(pl.multiple_of(base, 16), piece.shape[0]), :]
        return pltpu.make_async_copy(piece, target, sems.at[k])

    @pl.when(core == 0)
    def _():
        for side in range(kept):
            for j in range(steps):
                load(side, j).start()

    @pl.when(core != 0)
    def _():
        for side in reversed(range(kept)):
            for j in range(steps):
                load(side, j).start()

    rest_load = pltpu.make_async_copy(residual, start, sems.at[kept])
    rest_load.start()

    lane = lax.broadcasted_iota(jnp.int32, (16, width), 1)
    for t in range(kept * tiles):
        row = jnp.zeros((16, width), jnp.float32)
        for u in range(tiles):
            inside = (lane >= u * TILE) & (lane < (u + 1) * TILE)
            row = jnp.where(inside, mask[t * tiles + u].astype(jnp.float32), row)
        mask_rows[t] = row.astype(jnp.bfloat16)

    pairs = own.shape[0]
    peers, tall = swapped.shape[0], swapped.shape[1]
    rows = width // peers
    full = tall // rows
    half_rows = pairs // kept
    wide = 384
    stores = []

    def combine(d):
        count = min(LANES, pairs - d * LANES)
        if d < full:
            tile = swapped[:, d * rows : (d + 1) * rows, :].astype(jnp.float32)
        else:
            ends = swapped[:, d * rows :, :].astype(jnp.float32)
            low = ends[:, :8].reshape(peers * 8, LANES)
            middle = pltpu.roll(low, LANES // 2, 1).reshape(peers, 8, LANES)
            tile = jnp.concatenate([ends[:, :8], middle, ends[:, 8:]], axis=1)
        turned = jnp.transpose(tile.reshape(width, LANES))
        own_rows = own[d * LANES : d * LANES + count, :].astype(jnp.float32)
        combined[d * LANES : d * LANES + count, :] = (2.0 * own_rows - turned[:count]).astype(jnp.bfloat16)

    ready = 0
    for k in range(kept):
        while ready * LANES < (k + 1) * half_rows:
            combine(ready)
            ready += 1
        pltpu.make_async_copy(weights.at[k], weights.at[k], sems.at[k]).wait()
        if k == kept - 1:
            rest_load.wait()
        for n in range(width // wide):
            cols = slice(n * wide, (n + 1) * wide)
            masked = jnp.concatenate(
                [
                    weights[k, t * TILE : (t + 1) * TILE, cols].reshape(-1, 16, wide)
                    * mask_rows[k * tiles + t, :, cols][None]
                    for t in range(tiles)
                ]
            ).reshape(width, wide)
            total = jnp.dot(
                combined[k * half_rows : (k + 1) * half_rows, :], masked, preferred_element_type=jnp.float32
            )
            if k == 0:
                made[:, cols] = total
            else:
                made[:, cols] = made[:, cols] + total + start[:, cols]
                stores.append(pltpu.make_async_copy(made.at[:, cols], out.at[:, cols], sems.at[kept + 1 + n]))
                stores[-1].start()
    for store in stores:
        store.wait()


def final(where, mask, own, swapped, residual, pieces, kept):
    width = residual.shape[1]
    smem = pl.BlockSpec(memory_space=pltpu.SMEM)
    vmem = pl.BlockSpec(memory_space=pltpu.VMEM)
    hbm = pl.BlockSpec(memory_space=pltpu.HBM)
    return pl.pallas_call(
        final_body,
        in_specs=[smem] * 2 + [vmem] * 2 + [hbm] * (1 + len(pieces)),
        out_specs=hbm,
        out_shape=jax.ShapeDtypeStruct(residual.shape, jnp.float32),
        scratch_shapes=[
            pltpu.VMEM((kept, width, width), jnp.bfloat16),
            pltpu.VMEM(residual.shape, jnp.float32),
            pltpu.VMEM(own.shape, jnp.bfloat16),
            pltpu.VMEM(residual.shape, jnp.float32),
            pltpu.VMEM((kept * (width // TILE), 16, width), jnp.bfloat16),
            pltpu.SemaphoreType.DMA((kept + 1 + width // 384,)),
        ],
        compiler_params=pltpu.CompilerParams(vmem_limit_bytes=20 << 20),
        name="final",
    )(where, mask, own, swapped, in_hbm(residual), *[in_hbm(piece) for piece in pieces])


def per_device(amplitudes, integrals, block_mask, residual_in):
    kept, occ, rows, width = amplitudes.shape
    core = lax.rem(lax.axis_index("occ"), 2)
    column = lax.div(lax.axis_index("vir"), NZ)
    plane = lax.rem(lax.div(lax.axis_index("occ"), 2), 2)
    where = jnp.stack([core, column, plane]).astype(jnp.int32)

    along = NX * NZ
    occ_axis = lax.axis_size("occ")
    slab = jnp.where(core == 0, integrals[0], integrals[1])
    groups = [[x * NZ + z for z in range(NZ)] for x in range(NX)]
    here = lax.all_gather(slab, "vir", axis=0, tiled=True, axis_index_groups=groups)

    packed = pack(amplitudes.reshape(kept * occ, rows, width), here, width // rows)
    swapped = lax.all_to_all(packed, "vir", 0, 0, tiled=True)

    def neighbour(array, sign):
        pairs = [
            (o * along + v, o * along + (v + (NZ if o % 2 == 0 else -NZ) * sign) % along)
            for o in range(occ_axis)
            for v in range(along)
        ]
        return lax.ppermute(array, ("occ", "vir"), pairs)

    first = neighbour(here, 1)
    half = here.shape[0] // 2
    near = neighbour(lax.dynamic_slice_in_dim(here, plane * half, half, 0), -1)
    swap_cores = [(j, j ^ 1) for j in range(occ_axis)]
    across = lax.ppermute(here, "occ", swap_cores)
    first, near, across = lax.optimization_barrier((first, near, across))
    other = lax.ppermute(near, "occ", [(j, j ^ 2) for j in range(occ_axis)])
    pieces = [here, first, neighbour(first, 1), near, other]
    pieces += [across] + [lax.ppermute(piece, "occ", swap_cores) for piece in pieces[1:]]

    out = final(
        where,
        block_mask.reshape(-1),
        amplitudes.reshape(kept * occ * rows, width),
        swapped,
        residual_in.reshape(occ * rows, width),
        pieces,
        kept,
    )
    return out.reshape(residual_in.shape)


def solution(mesh):
    return jax.shard_map(
        per_device,
        mesh=mesh,
        in_specs=(P(None, "occ", "vir", None), P(None, "vir", None), P(), P("occ", "vir", None)),
        out_specs=P("occ", "vir", None),
        check_vma=False,
    )
```
